512 devices in a mesh: dp: 8 (over x, core), vocab: 64 (over y, z).
Axes of the slice: x: 4, y: 8, z: 8, core: 2. Of those that a mesh axis runs over, the one named last changes fastest.
Arguments:
- hidden: bfloat16 [640, 4608], P('dp'), may hold values from -30 to 30
- head_weight: bfloat16 [4608, 262144], P(None, ('dp', 'vocab')), may hold values from -0.09375 to 0.09375
- drafts: int32 [128, 4], replicated, may hold values from 0 to 262143
- cutoffs: int32 [128, 4], P('dp'), may hold values from -30720 to -18433
Outputs:
- log_norm: float32 [128, 5], P('dp')
- draft_logprob: float32 [128, 4], P('dp')
- expected_accept: float32 [128], P('dp')
- z_loss: float32 [], replicated
The draws below stay inside these ranges and needn't reach their ends.
All inputs are finite; a program needn't handle non-finite values.
Results may differ from the reference program's by a relative error of at most 0.0003.
Values may be sent and summed in bfloat16 or wider, within the bound.
A program may use at most 64 MiB of HBM per device.

```python
import jax
import jax.numpy as jnp
from jax import lax

D = 4608
V_DEV = 512
DRAFTS = 4
POSITIONS = 5
SEQS = 128
VOCAB = 262144
N_DP = 8
N_VOCAB = 64


def plant(result, key, low, largest):
    longest = result.shape.index(max(result.shape))
    spots = []
    for shift in (0, 1):
        where = [jax.random.randint(jax.random.fold_in(key, axis), (), 0, length) for axis, length in enumerate(result.shape)]
        where[longest] = (where[longest] + shift) % result.shape[longest]
        spots.append(tuple(where))
    return result.at[spots[0]].set(low).at[spots[1]].set(largest)


def block_scale(own_key, shape, shards, smallest, largest):
    def one(position, blocks):
        heights = jax.random.uniform(jax.random.fold_in(jax.random.fold_in(own_key, 6), position), (blocks,), jnp.float32, smallest / len(shards), largest / len(shards))
        return jnp.repeat(jnp.exp(heights), shape[position] // blocks).reshape((-1,) + (1,) * (len(shape) - position - 1))

    factor_of = one(*shards[0])
    for cut in shards[1:]:
        factor_of = factor_of * one(*cut)
    return factor_of


def normal_values(stream_key, extent, spread, most, pieces=(), kind=jnp.bfloat16):
    values = spread * jax.random.normal(stream_key, extent, jnp.float32)
    if pieces:
        values = values * block_scale(stream_key, extent, pieces, -0.22, 0.18)
    return jnp.clip(values, -most, most).astype(kind)


def setup_inputs(seed: int = 0) -> dict:
    keys = jax.random.split(jax.random.key(seed), 5)
    return {
        "hidden": normal_values(keys[0], (SEQS * POSITIONS, D), 5.0, 30.0, ((0, 8),)),
        "head_weight": normal_values(keys[1], (D, VOCAB), D ** -0.5, 0.09375, ((1, 512),)),
        "drafts": plant(jax.random.randint(keys[2], (SEQS, DRAFTS), 0, VOCAB), jax.random.fold_in(keys[2], 1), 0, VOCAB - 1).astype(jnp.int32),
        "cutoffs": plant(jax.random.randint(keys[3], (SEQS, DRAFTS), -30720, -18432), jax.random.fold_in(keys[3], 1), -30720, (-18432) - 1).astype(jnp.int32),
    }


SOFT_CAP = 30.0
Z_WEIGHT = 0.001


def reference(hidden, head_weight, drafts, cutoffs):
    stride = V_DEV * N_VOCAB
    sentinel = jnp.full((drafts.shape[0], 1), -1, jnp.int32)
    draft_rows = jnp.concatenate([drafts, sentinel], axis=1).reshape(-1)
    columns = lax.broadcasted_iota(jnp.int32, (1, stride), 1)

    def accumulate(carry, block):
        exp_total, picked = carry
        weights = lax.dynamic_slice_in_dim(head_weight, (block * stride).astype(jnp.int32), stride, 1)
        logits = jnp.dot(hidden, weights, preferred_element_type=jnp.float32)
        capped = SOFT_CAP * jnp.tanh(logits / SOFT_CAP)
        exp_total = exp_total + jnp.sum(jnp.exp(capped), axis=1)
        target = draft_rows - (block * stride).astype(jnp.int32)
        picked = picked + jnp.sum(jnp.where(columns == target[:, None], capped, jnp.zeros_like(capped)), axis=1)
        return (exp_total, picked), None

    zeros = jnp.zeros((hidden.shape[0],), jnp.float32)
    (exp_total, picked), unused = lax.scan(accumulate, (zeros, zeros), jnp.arange(N_DP, dtype=jnp.int32))
    log_total = jnp.log(exp_total)
    z_loss = Z_WEIGHT * jnp.mean(log_total * log_total)
    log_norm = log_total.reshape(-1, POSITIONS)
    picks = picked.reshape(-1, POSITIONS)
    draft_logprob = picks[:, :DRAFTS] - log_norm[:, :DRAFTS]
    accept = jax.nn.sigmoid(draft_logprob - cutoffs.astype(jnp.float32) / 1024.0)
    expected_accept = jnp.sum(jnp.cumprod(accept, axis=1), axis=1)
    return log_norm, draft_logprob, expected_accept, z_loss
```

```python
import functools

import jax
import jax.numpy as jnp
from jax import lax
from jax.experimental import pallas as pl
from jax.experimental.pallas import tpu as pltpu
from jax.sharding import Mesh
from jax.sharding import PartitionSpec as P

DRAFTS = 4
POSITIONS = 5
AXES = ("x", "core", "y", "z")
NX, NY, NZ = 4, 8, 8
MESH = pl.DeviceIdType.MESH

SOFT_CAP = 30.0
Z_WEIGHT = 0.001

ROWS = 80
WIDTH = 512
TILE = 256
TILES = 18
REGION = 3
DIRECT = 4 * REGION
GROUP = 3


def column_to_row(column, rows):
    at = lax.broadcasted_iota(jnp.int32, (rows, 128), 0)
    lane = lax.broadcasted_iota(jnp.int32, (rows, 128), 1)
    return jnp.sum(jnp.where(at == lane, column, 0.0), axis=0, keepdims=True)


def verify_kernel(
    hidden, weight, drafts, out,
    held, own_w, partner_w, acc_own, acc_partner, ids, part, z_in, plane, xy_in, log_part, log_in,
    load_sem, w_sem, w_send, w_recv, color_recv, color_send, direct_recv, direct_send,
    y_recv, z_recv, plane_send, red_send, red_recv, fin_send, fin_recv,
):
    x, core, y, z = (lax.axis_index(a) for a in AXES)
    step = 1 - 2 * core

    def ahead(n):
        return lax.rem(x + n * step + NX, NX)

    def at(dx=0, dy=0, dz=0):
        return (
            ahead(dx) if dx else x,
            core,
            lax.rem(y + dy + NY, NY) if dy else y,
            lax.rem(z + dz + NZ, NZ) if dz else z,
        )

    partner = (x, 1 - core, y, z)
    colour = lax.rem(y + 2 * z, 4)
    mine = REGION * colour

    def remote(src, dst, send, recv, to):
        copy = pltpu.make_async_remote_copy(
            src_ref=src, dst_ref=dst, send_sem=send, recv_sem=recv, device_id=to, device_id_type=MESH
        )
        copy.start()
        return copy

    for t in range(TILES):
        pltpu.make_async_copy(hidden.at[:, pl.ds(t * TILE, TILE)], held.at[t, 0], load_sem).start()
    load_w = pltpu.make_async_copy(weight, own_w, w_sem)
    load_w.start()

    barrier = pltpu.get_barrier_semaphore()
    peers = [at(dz=d) for d in range(1, NZ)]
    peers += [at(dx=a, dy=b) for a in range(NX) for b in range(NY) if a or b]
    peers.append(partner)
    for peer in peers:
        pl.semaphore_signal(barrier, inc=1, device_id=peer, device_id_type=MESH)
    pl.semaphore_wait(barrier, len(peers))

    pltpu.make_async_copy(held.at[:, 0], held.at[:, 0], load_sem).wait()
    sent = []
    front, back = at(dx=1), at(dx=-1)

    slots = {}
    for i, (to, slot, t) in enumerate(
        [(front, 1, 0), (back, 3, 2), (front, 1, 1), (back, 3, 0), (front, 1, 2), (back, 3, 1)]
    ):
        copy = remote(held.at[mine + t, 0], held.at[mine + t, slot], color_send.at[i], color_recv.at[i], to)
        slots[slot, t] = copy
        sent.append(copy)

    def direct(i, to, source, slot, first):
        tiles = pl.ds(first, GROUP)
        copy = remote(held.at[tiles, source], held.at[tiles, slot], direct_send.at[i], direct_recv.at[i], to)
        sent.append(copy)
        return copy

    low, high = DIRECT, DIRECT + GROUP
    direct_in = [direct(0, front, 0, 1, low), direct(1, back, 0, 3, high)]
    w_copy = remote(weight, partner_w, w_send, w_recv, partner)
    sent.append(w_copy)

    row = lax.broadcasted_iota(jnp.int32, (ROWS, 128), 0)
    lane = lax.broadcasted_iota(jnp.int32, (ROWS, 128), 1)
    for slot in range(NX):
        block = 2 * ahead(-slot) + core if slot else 2 * x + core
        chosen = drafts[pl.ds(pl.multiple_of(16 * block, 16), 16), :].astype(jnp.float32)
        spread = jnp.zeros((ROWS, 128), jnp.float32)
        for p in range(DRAFTS):
            here = row == lane * POSITIONS + p
            spread += jnp.where(here, column_to_row(chosen[:, p : p + 1], 16), 0.0)
        found = jnp.sum(spread, axis=1, keepdims=True)
        bonus = lax.rem(lax.broadcasted_iota(jnp.int32, (ROWS, 1), 0), POSITIONS) == DRAFTS
        ids[slot] = jnp.broadcast_to(jnp.where(bonus, -1.0, found), (ROWS, 128))

    plane_count = [0]

    def forward(slot, t):
        piece = held.at[mine + t, slot]
        toward = at(dz=1) if t < 2 else at(dz=-1)
        for to, sem in ((at(dy=1), y_recv.at[0, t]), (at(dy=-1), y_recv.at[1, t]), (toward, z_recv.at[t])):
            sent.append(remote(piece, piece, plane_send.at[plane_count[0]], sem, to))
            plane_count[0] += 1

    relays = {(1, 0): front, (3, 2): back, (1, 1): front}
    for slot, t in [(1, 0), (3, 2), (1, 1), (3, 0), (1, 2), (3, 1)]:
        slots[slot, t].wait_recv()
        if (slot, t) in relays:
            i = 6 + t
            copy = remote(
                held.at[mine + t, slot], held.at[mine + t, 2], color_send.at[i], color_recv.at[i], relays[slot, t]
            )
            slots[2, t] = copy
            sent.append(copy)
        forward(slot, t)
    direct_in += [direct(2, front, 0, 1, high), direct(3, back, 0, 3, low)]
    direct_in[0].wait_recv()
    direct_in.append(direct(4, front, 1, 2, low))
    direct_in[1].wait_recv()
    direct_in.append(direct(5, back, 3, 2, high))
    for t in (0, 2, 1):
        slots[2, t].wait_recv()
        forward(2, t)

    load_w.wait()
    w_copy.wait_recv()

    def multiply(first, start=False):
        for weights, total in ((own_w, acc_own), (partner_w, acc_partner)):
            value = None if start else total[...]
            for t in range(REGION):
                rows = pl.ds(pl.multiple_of((first + t) * TILE, TILE), TILE)
                product = jnp.dot(
                    held[first + t].reshape(NX * ROWS, TILE),
                    weights[rows, :],
                    preferred_element_type=jnp.float32,
                )
                value = product if value is None else value + product
            total[...] = value

    def arrived(first, t, sem):
        piece = held.at[first + t, pl.ds(1, NX - 1)]
        pltpu.make_async_copy(piece, piece, sem).wait()

    multiply(mine, start=True)
    other = REGION * lax.rem(colour + 2, 4)
    for t in range(REGION):
        arrived(other, t, z_recv.at[t])
    multiply(other)
    direct_in[3].wait_recv()
    direct_in[4].wait_recv()
    multiply(low)
    direct_in[2].wait_recv()
    direct_in[5].wait_recv()
    multiply(high)
    for k, shift in ((0, 3), (1, 1)):
        other = REGION * lax.rem(colour + shift, 4)
        for t in range(REGION):
            arrived(other, t, y_recv.at[k, t])
        multiply(other)

    vocab = y * NZ + z
    columns = lax.broadcasted_iota(jnp.int32, (ROWS, 128), 1)
    for slot in range(NX):
        exp_sum = jnp.zeros((ROWS, 128), jnp.float32)
        pick_sum = jnp.zeros((ROWS, 128), jnp.float32)
        wanted = ids[slot].astype(jnp.int32)
        for total, at_core in ((acc_own, core), (acc_partner, 1 - core)):
            offset = ((2 * x + at_core) * (NY * NZ) + vocab) * WIDTH
            for j in range(WIDTH // 128):
                logits = total[pl.ds(slot * ROWS, ROWS), pl.ds(j * 128, 128)]
                capped = SOFT_CAP * jnp.tanh(logits * (1.0 / SOFT_CAP))
                exp_sum += jnp.exp(capped)
                pick_sum += jnp.where(columns + (offset + j * 128) == wanted, capped, 0.0)
        part[pl.ds(slot, 1), :] = column_to_row(jnp.sum(exp_sum, axis=1, keepdims=True), ROWS)
        part[pl.ds(NX + slot, 1), :] = column_to_row(jnp.sum(pick_sum, axis=1, keepdims=True), ROWS)

    for d in range(1, NZ):
        remote(part, z_in.at[d - 1], red_send.at[0], red_recv.at[0], at(dz=d))
    pltpu.make_async_copy(z_in, z_in, red_recv.at[0]).wait()
    plane[...] = part[...] + jnp.sum(z_in[...], axis=0)
    n = NX * NY - 1
    for a in range(NX):
        for b in range(NY):
            if a or b:
                remote(plane, xy_in.at[a * NY + b - 1], red_send.at[1], red_recv.at[1], at(dx=a, dy=b))
    pltpu.make_async_copy(xy_in, xy_in, red_recv.at[1]).wait()
    from_x = []
    for a in range(NX):
        first = max(a * NY - 1, 0)
        count = NY if a else NY - 1
        value = jnp.sum(xy_in[pl.ds(first, count)], axis=0)
        from_x.append(value + plane[...] if a == 0 else value)
    totals = []
    for slot in range(NX):
        value = from_x[0][slot : slot + 1]
        for a in range(1, NX):
            k = (slot - a) % NX
            value += from_x[a][k : k + 1]
        totals.append(value)
    picked = from_x[0][NX : NX + 1]
    for a in range(1, NX):
        k = NX + (-a) % NX
        picked += from_x[a][k : k + 1]
    valid = lax.broadcasted_iota(jnp.int32, (1, 128), 1) < ROWS
    logs = [jnp.log(jnp.where(valid, value, 1.0)) for value in totals]
    squares = functools.reduce(jnp.add, [value * value for value in logs])
    log_part[...] = jnp.broadcast_to(squares, (8, 128))
    fin = remote(log_part, log_in, fin_send, fin_recv, partner)
    out[pl.ds(0, 1), :] = logs[0]
    out[pl.ds(1, 1), :] = picked
    fin.wait_recv()
    out[pl.ds(2, 1), :] = squares + log_in[pl.ds(0, 1), :]
    out[pl.ds(3, 5), :] = jnp.zeros((5, 128), jnp.float32)

    fin.wait_send()
    pltpu.make_async_copy(z_in, z_in, red_send.at[0]).wait()
    pltpu.make_async_copy(xy_in, xy_in, red_send.at[1]).wait()
    for copy in sent:
        copy.wait_send()


def finish_kernel(packed, cutoffs, log_norm, draft_logprob, expected, z_loss):
    seqs = 16
    at = lax.broadcasted_iota(jnp.int32, (seqs, 128), 0)
    lane = lax.broadcasted_iota(jnp.int32, (seqs, 128), 1)
    logs, picked, squares = packed[0:1], packed[1:2], packed[2:3]
    limits = cutoffs[...].astype(jnp.float32) * (1.0 / 1024.0)
    product = jnp.ones((seqs, 1), jnp.float32)
    total = jnp.zeros((seqs, 1), jnp.float32)
    for p in range(POSITIONS):
        here = lane == at * POSITIONS + p
        log_p = jnp.sum(jnp.where(here, logs, 0.0), axis=1, keepdims=True)
        log_norm[:, p : p + 1] = log_p
        if p < DRAFTS:
            draft = jnp.sum(jnp.where(here, picked, 0.0), axis=1, keepdims=True) - log_p
            draft_logprob[:, p : p + 1] = draft
            product = product * (1.0 / (1.0 + jnp.exp(limits[:, p : p + 1] - draft)))
            total = total + product
    expected[...] = column_to_row(total, seqs)[:, 0:seqs]
    z_loss[...] = jnp.sum(squares, axis=1, keepdims=True) * (Z_WEIGHT / (128 * POSITIONS))


def local(hidden, head_weight, drafts, cutoffs):
    f32, bf16 = jnp.float32, jnp.bfloat16
    dma = pltpu.SemaphoreType.DMA
    vmem = pl.BlockSpec(memory_space=pltpu.VMEM)
    hbm = pl.BlockSpec(memory_space=pl.ANY)
    packed = pl.pallas_call(
        verify_kernel,
        out_shape=jax.ShapeDtypeStruct((8, 128), f32),
        in_specs=[hbm, hbm, vmem],
        out_specs=vmem,
        scratch_shapes=[
            pltpu.VMEM((TILES, NX, ROWS, TILE), bf16),
            pltpu.VMEM((TILES * TILE, WIDTH), bf16),
            pltpu.VMEM((TILES * TILE, WIDTH), bf16),
            pltpu.VMEM((NX * ROWS, WIDTH), f32),
            pltpu.VMEM((NX * ROWS, WIDTH), f32),
            pltpu.VMEM((NX, ROWS, 128), f32),
            pltpu.VMEM((8, 128), f32),
            pltpu.VMEM((NZ - 1, 8, 128), f32),
            pltpu.VMEM((8, 128), f32),
            pltpu.VMEM((NX * NY - 1, 8, 128), f32),
            pltpu.VMEM((8, 128), f32),
            pltpu.VMEM((8, 128), f32),
            dma, dma, dma, dma,
            dma((9,)), dma((9,)), dma((6,)), dma((6,)),
            dma((2, REGION)), dma((REGION,)), dma((27,)),
            dma((2,)), dma((2,)), dma, dma,
        ],
        compiler_params=pltpu.CompilerParams(
            collective_id=0, has_side_effects=True, vmem_limit_bytes=60 * 2**20
        ),
        name="verify",
    )(hidden, head_weight, drafts)
    log_norm, draft_logprob, expected, z_loss = pl.pallas_call(
        finish_kernel,
        out_shape=[
            jax.ShapeDtypeStruct((16, POSITIONS), f32),
            jax.ShapeDtypeStruct((16, DRAFTS), f32),
            jax.ShapeDtypeStruct((1, 16), f32),
            jax.ShapeDtypeStruct((1, 1), f32),
        ],
        in_specs=[vmem, vmem],
        out_specs=[vmem] * 4,
        name="finish",
    )(packed, cutoffs)
    return log_norm, draft_logprob, expected.reshape(16), z_loss.reshape(())


def solution(mesh):
    split = Mesh(mesh.devices.reshape(NX, 2, NY, NZ), AXES)
    dp, everything = ("x", "core"), ("x", "core", "y", "z")
    return jax.shard_map(
        local,
        mesh=split,
        in_specs=(P(dp, None), P(None, everything), P(), P(dp, None)),
        out_specs=(P(dp, None), P(dp, None), P(dp), P()),
        check_vma=False,
    )
```

```python
import functools

import jax
import jax.numpy as jnp
from jax import lax
from jax.experimental import pallas as pl
from jax.experimental.pallas import tpu as pltpu
from jax.sharding import Mesh
from jax.sharding import PartitionSpec as P

DRAFTS = 4
POSITIONS = 5
AXES = ("x", "core", "y", "z")
NX, NY, NZ = 4, 8, 8
MESH = pl.DeviceIdType.MESH

SOFT_CAP = 30.0
Z_WEIGHT = 0.001

ROWS = 80
WIDTH = 512
TILE = 256
TILES = 18
REGION = 3
DIRECT = 4 * REGION
BEHIND = (0, 1, 3, 2)


def column_to_row(column, rows):
    at = lax.broadcasted_iota(jnp.int32, (rows, 128), 0)
    lane = lax.broadcasted_iota(jnp.int32, (rows, 128), 1)
    return jnp.sum(jnp.where(at == lane, column, 0.0), axis=0, keepdims=True)


def verify_kernel(
    hidden, weight, drafts, out,
    held, own_w, partner_w, acc_own, acc_partner, wanted, ids, part, z_in, xy_out, xy_in, log_part, log_in,
    load_sem, small_sem, w_sem, w_send, w_recv, color_recv, color_send, direct_recv, direct_send,
    near_recv, far_recv, plane_send, red_send, red_recv, fin_send, fin_recv, round_a, round_b, round_c,
):
    x, core, y, z = (lax.axis_index(a) for a in AXES)
    step = 1 - 2 * core

    def ahead(n):
        return lax.rem(x + n * step + NX, NX)

    def at(dx=0, dy=0, dz=0):
        return (
            ahead(dx) if dx else x,
            core,
            lax.rem(y + dy + NY, NY) if dy else y,
            lax.rem(z + dz + NZ, NZ) if dz else z,
        )

    partner = (x, 1 - core, y, z)
    front, back = at(dx=1), at(dx=-1)
    colour = lax.rem(y + 2 * z, 4)
    mine = REGION * colour
    sent = []

    def remote(src, dst, send, recv, to):
        copy = pltpu.make_async_remote_copy(
            src_ref=src, dst_ref=dst, send_sem=send, recv_sem=recv, device_id=to, device_id_type=MESH
        )
        copy.start()
        return copy

    def signal(sem, peers):
        for peer in peers:
            pl.semaphore_signal(sem, inc=1, device_id=peer, device_id_type=MESH)
        return len(peers)

    neighbours = [front, back, at(dy=1), at(dy=-1), at(dz=1), at(dz=-1)]
    barrier = pltpu.get_barrier_semaphore()
    greeted = signal(barrier, neighbours + [partner])

    for t in range(TILES):
        pltpu.make_async_copy(hidden.at[:, pl.ds(t * TILE, TILE)], held.at[t, 0], load_sem).start()
    load_ids = pltpu.make_async_copy(drafts, wanted, small_sem)
    load_ids.start()
    load_w = pltpu.make_async_copy(weight, own_w, w_sem)
    load_w.start()
    pltpu.make_async_copy(held.at[:, 0], held.at[:, 0], load_sem).wait()
    pl.semaphore_wait(barrier, greeted)

    color_in = {}
    for i, (to, place, t) in enumerate(
        [(front, 1, 0), (back, 2, 2), (front, 1, 1), (back, 2, 0), (front, 1, 2), (back, 2, 1)]
    ):
        copy = remote(held.at[mine + t, 0], held.at[mine + t, place], color_send.at[i], color_recv.at[i], to)
        color_in[place, t] = copy
        sent.append(copy)

    direct_in = {}

    def direct(to, source, place, t):
        i = len(direct_in)
        copy = remote(
            held.at[DIRECT + t, source], held.at[DIRECT + t, place], direct_send.at[i], direct_recv.at[i], to
        )
        direct_in[place, t] = copy
        sent.append(copy)

    low, high = range(REGION), range(REGION, 2 * REGION)
    for i in range(REGION):
        direct(front, 0, 1, low[i])
        direct(back, 0, 2, high[i])
    w_copy = remote(weight, partner_w, w_send, w_recv, partner)
    sent.append(w_copy)

    signal(round_a, neighbours)

    load_ids.wait()
    row = lax.broadcasted_iota(jnp.int32, (ROWS, 128), 0)
    lane = lax.broadcasted_iota(jnp.int32, (ROWS, 128), 1)
    chosen = wanted[...].astype(jnp.float32)
    bonus = lax.rem(lax.broadcasted_iota(jnp.int32, (ROWS, 1), 0), POSITIONS) == DRAFTS
    for place in range(NX):
        block = 2 * ahead(-BEHIND[place]) + core
        spread = jnp.zeros((ROWS, 128), jnp.float32)
        for p in range(DRAFTS):
            here = row + ROWS * block == lane * POSITIONS + p
            spread += jnp.where(here, chosen[p : p + 1], 0.0)
        found = jnp.sum(spread, axis=1, keepdims=True)
        ids[place] = jnp.broadcast_to(jnp.where(bonus, -1.0, found), (ROWS, 128)).astype(jnp.int32)

    plane_count = [0]

    def forward(place, t):
        piece = held.at[mine + t, place]
        toward = at(dz=1) if t < 2 else at(dz=-1)
        recv = far_recv if place == 3 else near_recv
        for k, to in ((0, at(dy=1)), (1, at(dy=-1)), (2, toward)):
            sent.append(remote(piece, piece, plane_send.at[plane_count[0]], recv.at[k, t], to))
            plane_count[0] += 1

    relays = {(1, 0): front, (2, 2): back, (1, 1): front}
    for place, t in [(1, 0), (2, 2), (1, 1), (2, 0), (1, 2), (2, 1)]:
        color_in[place, t].wait_recv()
        if (place, t) in relays:
            i = 6 + t
            copy = remote(
                held.at[mine + t, place], held.at[mine + t, 3], color_send.at[i], color_recv.at[i], relays[place, t]
            )
            color_in[3, t] = copy
            sent.append(copy)
        forward(place, t)
    for i in range(REGION):
        direct(front, 0, 1, high[i])
        direct(back, 0, 2, low[i])
    pl.semaphore_wait(round_a, len(neighbours))
    count_b = signal(round_b, [at(dy=2), at(dy=-2), at(dz=2), at(dz=-2)])
    for i in range(REGION):
        direct_in[1, low[i]].wait_recv()
        direct(front, 1, 3, low[i])
        direct_in[2, high[i]].wait_recv()
        direct(back, 2, 3, high[i])
    for t in (0, 2, 1):
        color_in[3, t].wait_recv()
        forward(3, t)
    pl.semaphore_wait(round_b, count_b)
    count_c = signal(round_c, [at(dx=1), at(dx=-1), at(dx=2)])

    load_w.wait()
    w_copy.wait_recv()
    near, far = (0, 3), (3, 1)

    def multiply(span, tiles, start=False):
        first, count = span
        rows = pl.ds(first * ROWS, count * ROWS)
        for weights, total in ((own_w, acc_own), (partner_w, acc_partner)):
            value = None if start else total[rows, :]
            for t in tiles:
                depth = pl.ds(pl.multiple_of(t * TILE, TILE), TILE)
                product = jnp.dot(
                    held[t, pl.ds(first, count)].reshape(count * ROWS, TILE),
                    weights[depth, :],
                    preferred_element_type=jnp.float32,
                )
                value = product if value is None else value + product
            total[rows, :] = value

    def arrived(t, span, sem):
        piece = held.at[t, pl.ds(*span)]
        pltpu.make_async_copy(piece, piece, sem).wait()

    vocab = y * NZ + z
    columns = lax.broadcasted_iota(jnp.int32, (ROWS, 128), 1)

    def summed(place):
        exp_sum = jnp.zeros((ROWS, 128), jnp.float32)
        pick_sum = jnp.zeros((ROWS, 128), jnp.float32)
        for total, at_core in ((acc_own, core), (acc_partner, 1 - core)):
            offset = ((2 * x + at_core) * (NY * NZ) + vocab) * WIDTH
            for j in range(WIDTH // 128):
                logits = total[pl.ds(place * ROWS, ROWS), pl.ds(j * 128, 128)]
                capped = SOFT_CAP * jnp.tanh(logits * (1.0 / SOFT_CAP))
                exp_sum += jnp.exp(capped)
                pick_sum += jnp.where(columns + (offset + j * 128) == ids[place], capped, 0.0)
        k = BEHIND[place]
        part[pl.ds(k, 1), :] = column_to_row(jnp.sum(exp_sum, axis=1, keepdims=True), ROWS)
        part[pl.ds(NX + k, 1), :] = column_to_row(jnp.sum(pick_sum, axis=1, keepdims=True), ROWS)

    def region(shift):
        return REGION * lax.rem(colour + shift, 4)

    own_tiles = [mine + t for t in range(REGION)]
    multiply(near, own_tiles, start=True)
    multiply(far, own_tiles, start=True)
    sides = ((2, 2), (0, 3), (1, 1))
    for k, shift in sides:
        tiles = [region(shift) + t for t in range(REGION)]
        for t in range(REGION):
            arrived(tiles[t], (1, 2), near_recv.at[k, t])
        multiply(near, tiles)
    for group, place in ((low, 2), (high, 1)):
        for t in group:
            direct_in[place, t].wait_recv()
        multiply(near, [DIRECT + t for t in group])
    tiles = [region(2) + t for t in range(REGION)]
    for t in range(REGION):
        arrived(tiles[t], (3, 1), far_recv.at[2, t])
    multiply(far, tiles)
    pl.semaphore_wait(round_c, count_c)
    for place in (0, 1, 2):
        summed(place)
    for i, t in enumerate((0, 2, 1)):
        tiles = []
        for group in (low, high):
            direct_in[3, group[i]].wait_recv()
            tiles.append(DIRECT + group[i])
        for k, shift in sides[1:]:
            tiles.append(region(shift) + t)
            arrived(tiles[-1], (3, 1), far_recv.at[k, t])
        multiply(far, tiles)
    summed(3)

    for d in range(1, NZ):
        remote(part, z_in.at[d - 1], red_send.at[0], red_recv.at[0], at(dz=d))
    pltpu.make_async_copy(z_in, z_in, red_recv.at[0]).wait()
    plane = part[...] + jnp.sum(z_in[...], axis=0)
    for a in range(NX):
        k = NX + (-a) % NX
        xy_out[a, 0:NX] = plane[0:NX]
        xy_out[a, NX : NX + 1] = plane[k : k + 1]
    used = pl.ds(0, NX + 1)
    for a in range(NX):
        for b in range(NY):
            if a or b:
                remote(
                    xy_out.at[a, used], xy_in.at[a * NY + b - 1, used], red_send.at[1], red_recv.at[1], at(dx=a, dy=b)
                )
    pltpu.make_async_copy(xy_in.at[:, used], xy_in.at[:, used], red_recv.at[1]).wait()
    from_x = []
    for a in range(NX):
        first = max(a * NY - 1, 0)
        count = NY if a else NY - 1
        value = jnp.sum(xy_in[pl.ds(first, count), 0 : NX + 1], axis=0)
        from_x.append(value + xy_out[0, 0 : NX + 1] if a == 0 else value)
    totals = []
    for slot in range(NX):
        value = from_x[0][slot : slot + 1]
        for a in range(1, NX):
            k = (slot - a) % NX
            value += from_x[a][k : k + 1]
        totals.append(value)
    picked = functools.reduce(jnp.add, [value[NX : NX + 1] for value in from_x])
    valid = lax.broadcasted_iota(jnp.int32, (1, 128), 1) < ROWS
    logs = [jnp.log(jnp.where(valid, value, 1.0)) for value in totals]
    squares = functools.reduce(jnp.add, [value * value for value in logs])
    log_part[...] = jnp.broadcast_to(squares, (8, 128))
    fin = remote(log_part, log_in, fin_send, fin_recv, partner)
    out[pl.ds(0, 1), :] = logs[0]
    out[pl.ds(1, 1), :] = picked
    out[pl.ds(3, 5), :] = jnp.zeros((5, 128), jnp.float32)
    pltpu.make_async_copy(z_in, z_in, red_send.at[0]).wait()
    pltpu.make_async_copy(xy_in.at[:, used], xy_in.at[:, used], red_send.at[1]).wait()
    for copy in sent:
        copy.wait_send()
    fin.wait()
    out[pl.ds(2, 1), :] = squares + log_in[pl.ds(0, 1), :]


def finish_kernel(packed, cutoffs, log_norm, draft_logprob, expected, z_loss):
    seqs = 16
    at = lax.broadcasted_iota(jnp.int32, (seqs, 128), 0)
    lane = lax.broadcasted_iota(jnp.int32, (seqs, 128), 1)
    logs, picked, squares = packed[0:1], packed[1:2], packed[2:3]
    product = jnp.ones((1, seqs), jnp.float32)
    total = jnp.zeros((1, seqs), jnp.float32)
    for p in range(POSITIONS):
        here = lane == at * POSITIONS + p

        def of(values):
            return column_to_row(jnp.sum(jnp.where(here, values, 0.0), axis=1, keepdims=True), seqs)[:, 0:seqs]

        log_p = of(logs)
        log_norm[p : p + 1, :] = log_p
        if p < DRAFTS:
            draft = of(picked) - log_p
            draft_logprob[p : p + 1, :] = draft
            limit = cutoffs[p : p + 1, :].astype(jnp.float32) * (1.0 / 1024.0)
            product = product * (1.0 / (1.0 + jnp.exp(limit - draft)))
            total = total + product
    expected[...] = total
    z_loss[...] = jnp.sum(squares, axis=1, keepdims=True) * (Z_WEIGHT / (128 * POSITIONS))


def local(hidden, head_weight, drafts, cutoffs):
    f32, bf16 = jnp.float32, jnp.bfloat16
    dma, regular = pltpu.SemaphoreType.DMA, pltpu.SemaphoreType.REGULAR
    vmem = pl.BlockSpec(memory_space=pltpu.VMEM)
    hbm = pl.BlockSpec(memory_space=pl.ANY)
    packed = pl.pallas_call(
        verify_kernel,
        out_shape=jax.ShapeDtypeStruct((8, 128), f32),
        in_specs=[hbm, hbm, hbm],
        out_specs=vmem,
        scratch_shapes=[
            pltpu.VMEM((TILES, NX, ROWS, TILE), bf16),
            pltpu.VMEM((TILES * TILE, WIDTH), bf16),
            pltpu.VMEM((TILES * TILE, WIDTH), bf16),
            pltpu.VMEM((NX * ROWS, WIDTH), f32),
            pltpu.VMEM((NX * ROWS, WIDTH), f32),
            pltpu.VMEM((DRAFTS, 128), jnp.int32),
            pltpu.VMEM((NX, ROWS, 128), jnp.int32),
            pltpu.VMEM((8, 128), f32),
            pltpu.VMEM((NZ - 1, 8, 128), f32),
            pltpu.VMEM((NX, 8, 128), f32),
            pltpu.VMEM((NX * NY - 1, 8, 128), f32),
            pltpu.VMEM((8, 128), f32),
            pltpu.VMEM((8, 128), f32),
            dma, dma, dma, dma, dma,
            dma((9,)), dma((9,)), dma((18,)), dma((18,)),
            dma((3, REGION)), dma((3, REGION)), dma((27,)),
            dma((2,)), dma((2,)), dma, dma,
            regular, regular, regular,
        ],
        compiler_params=pltpu.CompilerParams(
            collective_id=0, has_side_effects=True, vmem_limit_bytes=60 * 2**20
        ),
        name="verify",
    )(hidden, head_weight, drafts.T)
    log_norm, draft_logprob, expected, z_loss = pl.pallas_call(
        finish_kernel,
        out_shape=[
            jax.ShapeDtypeStruct((POSITIONS, 16), f32),
            jax.ShapeDtypeStruct((DRAFTS, 16), f32),
            jax.ShapeDtypeStruct((1, 16), f32),
            jax.ShapeDtypeStruct((1, 1), f32),
        ],
        in_specs=[vmem, vmem],
        out_specs=[vmem] * 4,
        name="finish",
    )(packed, cutoffs.T)
    return log_norm.T, draft_logprob.T, expected.reshape(16), z_loss.reshape(())


def solution(mesh):
    split = Mesh(mesh.devices.reshape(NX, 2, NY, NZ), AXES)
    dp, everything = ("x", "core"), ("x", "core", "y", "z")
    return jax.shard_map(
        local,
        mesh=split,
        in_specs=(P(dp, None), P(None, everything), P(), P(dp, None)),
        out_specs=(P(dp, None), P(dp, None), P(dp), P()),
        check_vma=False,
    )
```

```python
import functools

import jax
import jax.numpy as jnp
from jax import lax
from jax.experimental import pallas as pl
from jax.experimental.pallas import tpu as pltpu
from jax.sharding import Mesh
from jax.sharding import PartitionSpec as P

DRAFTS = 4
POSITIONS = 5
AXES = ("x", "core", "y", "z")
NX, NY, NZ = 4, 8, 8
MESH = pl.DeviceIdType.MESH

SOFT_CAP = 30.0
Z_WEIGHT = 0.001

ROWS = 80
WIDTH = 512
TILE = 256
TILES = 18
REGION = 3
DIRECT = 4 * REGION
PAIR = 2
BEHIND = (0, 1, 3, 2)


def column_to_row(column, rows):
    at = lax.broadcasted_iota(jnp.int32, (rows, 128), 0)
    lane = lax.broadcasted_iota(jnp.int32, (rows, 128), 1)
    return jnp.sum(jnp.where(at == lane, column, 0.0), axis=0, keepdims=True)


def verify_kernel(
    hidden, weight, drafts, out,
    held, own_w, partner_w, acc_own, acc_partner, wanted, ids, part, z_in, xy_out, xy_in, log_part, log_in,
    load_sem, small_sem, w_sem, w_send, w_recv, color_recv, color_send, direct_recv, direct_send,
    near_recv, far_recv, plane_send, shared_recv, shared_send, red_send, red_recv, fin_send, fin_recv, round_a, round_b, round_c,
):
    x, core, y, z = (lax.axis_index(a) for a in AXES)
    step = 1 - 2 * core

    def ahead(n):
        return lax.rem(x + n * step + NX, NX)

    def at(dx=0, dy=0, dz=0):
        return (
            ahead(dx) if dx else x,
            core,
            lax.rem(y + dy + NY, NY) if dy else y,
            lax.rem(z + dz + NZ, NZ) if dz else z,
        )

    partner = (x, 1 - core, y, z)
    front, back = at(dx=1), at(dx=-1)
    colour = lax.rem(y + 2 * z, 4)
    mine = REGION * colour
    sent = []

    def remote(src, dst, send, recv, to):
        copy = pltpu.make_async_remote_copy(
            src_ref=src, dst_ref=dst, send_sem=send, recv_sem=recv, device_id=to, device_id_type=MESH
        )
        copy.start()
        return copy

    def signal(sem, peers):
        for peer in peers:
            pl.semaphore_signal(sem, inc=1, device_id=peer, device_id_type=MESH)
        return len(peers)

    neighbours = [front, back, at(dy=1), at(dy=-1), at(dz=1), at(dz=-1)]
    barrier = pltpu.get_barrier_semaphore()
    greeted = signal(barrier, neighbours + [partner])

    for t in range(TILES):
        pltpu.make_async_copy(hidden.at[:, pl.ds(t * TILE, TILE)], held.at[t, 0], load_sem).start()
    load_ids = pltpu.make_async_copy(drafts, wanted, small_sem)
    load_ids.start()
    load_w = pltpu.make_async_copy(weight, own_w, w_sem)
    load_w.start()
    pltpu.make_async_copy(held.at[:, 0], held.at[:, 0], load_sem).wait()
    pl.semaphore_wait(barrier, greeted)

    color_in = {}
    for i, (to, place, t) in enumerate(
        [(front, 1, 0), (back, 2, 2), (front, 1, 1), (back, 2, 0), (front, 1, 2), (back, 2, 1)]
    ):
        copy = remote(held.at[mine + t, 0], held.at[mine + t, place], color_send.at[i], color_recv.at[i], to)
        color_in[place, t] = copy
        sent.append(copy)

    direct_in = {}

    def direct(to, source, place, t, key=None):
        i = len(direct_in)
        copy = remote(
            held.at[DIRECT + t, source], held.at[DIRECT + t, place], direct_send.at[i], direct_recv.at[i], to
        )
        direct_in[place, t if key is None else key] = copy
        sent.append(copy)

    parity = lax.rem(z, 2)
    over_x, over_z = 2 * PAIR + parity, 2 * PAIR + 1 - parity
    direct(front, 0, 1, over_x, "x")
    direct(back, 0, 2, over_x, "x")
    low, high = range(PAIR), range(PAIR, 2 * PAIR)
    for i in range(PAIR):
        direct(front, 0, 1, low[i])
        direct(back, 0, 2, high[i])
    w_copy = remote(weight, partner_w, w_send, w_recv, partner)
    sent.append(w_copy)

    signal(round_a, neighbours)

    load_ids.wait()
    row = lax.broadcasted_iota(jnp.int32, (ROWS, 128), 0)
    lane = lax.broadcasted_iota(jnp.int32, (ROWS, 128), 1)
    chosen = wanted[...].astype(jnp.float32)
    bonus = lax.rem(lax.broadcasted_iota(jnp.int32, (ROWS, 1), 0), POSITIONS) == DRAFTS
    for place in range(NX):
        block = 2 * ahead(-BEHIND[place]) + core
        spread = jnp.zeros((ROWS, 128), jnp.float32)
        for p in range(DRAFTS):
            here = row + ROWS * block == lane * POSITIONS + p
            spread += jnp.where(here, chosen[p : p + 1], 0.0)
        found = jnp.sum(spread, axis=1, keepdims=True)
        ids[place] = jnp.broadcast_to(jnp.where(bonus, -1.0, found), (ROWS, 128)).astype(jnp.int32)

    plane_count = [0]

    def forward(place, t):
        piece = held.at[mine + t, place]
        toward = at(dz=1) if t < 2 else at(dz=-1)
        recv = far_recv if place == 3 else near_recv
        for k, to in ((0, at(dy=1)), (1, at(dy=-1)), (2, toward)):
            sent.append(remote(piece, piece, plane_send.at[plane_count[0]], recv.at[k, t], to))
            plane_count[0] += 1

    relays = {(1, 0): front, (2, 2): back, (1, 1): front}
    for place, t in [(1, 0), (2, 2), (1, 1), (2, 0), (1, 2), (2, 1)]:
        color_in[place, t].wait_recv()
        if (place, t) in relays:
            i = 6 + t
            copy = remote(
                held.at[mine + t, place], held.at[mine + t, 3], color_send.at[i], color_recv.at[i], relays[place, t]
            )
            color_in[3, t] = copy
            sent.append(copy)
        forward(place, t)

    def share(place):
        piece = held.at[DIRECT + over_x, place]
        to = at(dz=-1) if place == 2 else at(dz=1)
        sent.append(remote(piece, piece, shared_send.at[place - 1], shared_recv.at[place - 1], to))

    direct_in[1, "x"].wait_recv()
    share(1)
    direct_in[2, "x"].wait_recv()
    direct(back, 2, 3, over_x, "x")
    share(2)
    for i in range(PAIR):
        direct(front, 0, 1, high[i])
        direct(back, 0, 2, low[i])
    pl.semaphore_wait(round_a, len(neighbours))
    count_b = signal(round_b, [at(dy=2), at(dy=-2), at(dz=2), at(dz=-2)])
    for i in range(PAIR):
        direct_in[1, low[i]].wait_recv()
        direct(front, 1, 3, low[i])
        direct_in[2, high[i]].wait_recv()
        direct(back, 2, 3, high[i])
    for t in (0, 2, 1):
        color_in[3, t].wait_recv()
        forward(3, t)
    direct_in[3, "x"].wait_recv()
    share(3)
    pl.semaphore_wait(round_b, count_b)
    count_c = signal(round_c, [at(dx=1), at(dx=-1), at(dx=2)])

    load_w.wait()
    w_copy.wait_recv()
    near, far = (0, 3), (3, 1)

    def multiply(span, tiles, start=False):
        first, count = span
        rows = pl.ds(first * ROWS, count * ROWS)
        for weights, total in ((own_w, acc_own), (partner_w, acc_partner)):
            value = None if start else total[rows, :]
            for t in tiles:
                depth = pl.ds(pl.multiple_of(t * TILE, TILE), TILE)
                product = jnp.dot(
                    held[t, pl.ds(first, count)].reshape(count * ROWS, TILE),
                    weights[depth, :],
                    preferred_element_type=jnp.float32,
                )
                value = product if value is None else value + product
            total[rows, :] = value

    def arrived(t, span, sem):
        piece = held.at[t, pl.ds(*span)]
        pltpu.make_async_copy(piece, piece, sem).wait()

    vocab = y * NZ + z
    columns = lax.broadcasted_iota(jnp.int32, (ROWS, 128), 1)

    def summed(place):
        exp_sum = jnp.zeros((ROWS, 128), jnp.float32)
        pick_sum = jnp.zeros((ROWS, 128), jnp.float32)
        for total, at_core in ((acc_own, core), (acc_partner, 1 - core)):
            offset = ((2 * x + at_core) * (NY * NZ) + vocab) * WIDTH
            for j in range(WIDTH // 128):
                logits = total[pl.ds(place * ROWS, ROWS), pl.ds(j * 128, 128)]
                capped = SOFT_CAP * jnp.tanh(logits * (1.0 / SOFT_CAP))
                exp_sum += jnp.exp(capped)
                pick_sum += jnp.where(columns + (offset + j * 128) == ids[place], capped, 0.0)
        k = BEHIND[place]
        part[pl.ds(k, 1), :] = column_to_row(jnp.sum(exp_sum, axis=1, keepdims=True), ROWS)
        part[pl.ds(NX + k, 1), :] = column_to_row(jnp.sum(pick_sum, axis=1, keepdims=True), ROWS)

    def region(shift):
        return REGION * lax.rem(colour + shift, 4)

    own_tiles = [mine + t for t in range(REGION)]
    multiply(near, own_tiles, start=True)
    multiply(far, own_tiles, start=True)
    sides = ((2, 2), (0, 3), (1, 1))
    for k, shift in sides:
        tiles = [region(shift) + t for t in range(REGION)]
        for t in range(REGION):
            arrived(tiles[t], (1, 2), near_recv.at[k, t])
        multiply(near, tiles)
    for place in (1, 2):
        arrived(DIRECT + over_z, (place, 1), shared_recv.at[place - 1])
    for group, place in ((low, 2), (high, 1)):
        for t in group:
            direct_in[place, t].wait_recv()
    multiply(near, [DIRECT + t for t in range(2 * PAIR + 2)])
    tiles = [region(2) + t for t in range(REGION)]
    for t in range(REGION):
        arrived(tiles[t], (3, 1), far_recv.at[2, t])
    multiply(far, tiles)
    pl.semaphore_wait(round_c, count_c)
    for place in (0, 1, 2):
        summed(place)
    for i, t in enumerate((0, 2, 1)):
        tiles = []
        for group in (low, high) if i < PAIR else ():
            direct_in[3, group[i]].wait_recv()
            tiles.append(DIRECT + group[i])
        if i == PAIR:
            arrived(DIRECT + over_z, (3, 1), shared_recv.at[2])
            tiles += [DIRECT + 2 * PAIR, DIRECT + 2 * PAIR + 1]
        for k, shift in sides[1:]:
            tiles.append(region(shift) + t)
            arrived(tiles[-1], (3, 1), far_recv.at[k, t])
        multiply(far, tiles)
    summed(3)

    for d in sorted(range(1, NZ), key=lambda d: -min(d, NZ - d)):
        remote(part, z_in.at[d - 1], red_send.at[0], red_recv.at[0], at(dz=d))
    pltpu.make_async_copy(z_in, z_in, red_recv.at[0]).wait()
    plane = part[...] + jnp.sum(z_in[...], axis=0)
    for a in range(NX):
        k = NX + (-a) % NX
        xy_out[a, 0:NX] = plane[0:NX]
        xy_out[a, NX : NX + 1] = plane[k : k + 1]
    used = pl.ds(0, NX + 1)
    pairs = [(a, b) for a in range(NX) for b in range(NY) if a or b]
    for a, b in sorted(pairs, key=lambda p: -min(p[0], NX - p[0]) - min(p[1], NY - p[1])):
        remote(xy_out.at[a, used], xy_in.at[a * NY + b - 1, used], red_send.at[1], red_recv.at[1], at(dx=a, dy=b))
    pltpu.make_async_copy(xy_in.at[:, used], xy_in.at[:, used], red_recv.at[1]).wait()
    from_x = []
    for a in range(NX):
        first = max(a * NY - 1, 0)
        count = NY if a else NY - 1
        value = jnp.sum(xy_in[pl.ds(first, count), 0 : NX + 1], axis=0)
        from_x.append(value + xy_out[0, 0 : NX + 1] if a == 0 else value)
    totals = []
    for slot in range(NX):
        value = from_x[0][slot : slot + 1]
        for a in range(1, NX):
            k = (slot - a) % NX
            value += from_x[a][k : k + 1]
        totals.append(value)
    picked = functools.reduce(jnp.add, [value[NX : NX + 1] for value in from_x])
    valid = lax.broadcasted_iota(jnp.int32, (1, 128), 1) < ROWS
    logs = [jnp.log(jnp.where(valid, value, 1.0)) for value in totals]
    squares = functools.reduce(jnp.add, [value * value for value in logs])
    log_part[...] = jnp.broadcast_to(squares, (8, 128))
    fin = remote(log_part, log_in, fin_send, fin_recv, partner)
    out[pl.ds(0, 1), :] = logs[0]
    out[pl.ds(1, 1), :] = picked
    out[pl.ds(3, 5), :] = jnp.zeros((5, 128), jnp.float32)
    pltpu.make_async_copy(z_in, z_in, red_send.at[0]).wait()
    pltpu.make_async_copy(xy_in.at[:, used], xy_in.at[:, used], red_send.at[1]).wait()
    for copy in sent:
        copy.wait_send()
    fin.wait()
    out[pl.ds(2, 1), :] = squares + log_in[pl.ds(0, 1), :]


def finish_kernel(packed, cutoffs, log_norm, draft_logprob, expected, z_loss):
    seqs = 16
    at = lax.broadcasted_iota(jnp.int32, (seqs, 128), 0)
    lane = lax.broadcasted_iota(jnp.int32, (seqs, 128), 1)
    logs, picked, squares = packed[0:1], packed[1:2], packed[2:3]
    product = jnp.ones((1, seqs), jnp.float32)
    total = jnp.zeros((1, seqs), jnp.float32)
    for p in range(POSITIONS):
        here = lane == at * POSITIONS + p

        def of(values):
            return column_to_row(jnp.sum(jnp.where(here, values, 0.0), axis=1, keepdims=True), seqs)[:, 0:seqs]

        log_p = of(logs)
        log_norm[p : p + 1, :] = log_p
        if p < DRAFTS:
            draft = of(picked) - log_p
            draft_logprob[p : p + 1, :] = draft
            limit = cutoffs[p : p + 1, :].astype(jnp.float32) * (1.0 / 1024.0)
            product = product * (1.0 / (1.0 + jnp.exp(limit - draft)))
            total = total + product
    expected[...] = total
    z_loss[...] = jnp.sum(squares, axis=1, keepdims=True) * (Z_WEIGHT / (128 * POSITIONS))


def local(hidden, head_weight, drafts, cutoffs):
    f32, bf16 = jnp.float32, jnp.bfloat16
    dma, regular = pltpu.SemaphoreType.DMA, pltpu.SemaphoreType.REGULAR
    vmem = pl.BlockSpec(memory_space=pltpu.VMEM)
    hbm = pl.BlockSpec(memory_space=pltpu.HBM)
    packed = pl.pallas_call(
        verify_kernel,
        out_shape=jax.ShapeDtypeStruct((8, 128), f32),
        in_specs=[hbm, hbm, hbm],
        out_specs=vmem,
        scratch_shapes=[
            pltpu.VMEM((TILES, NX, ROWS, TILE), bf16),
            pltpu.VMEM((TILES * TILE, WIDTH), bf16),
            pltpu.VMEM((TILES * TILE, WIDTH), bf16),
            pltpu.VMEM((NX * ROWS, WIDTH), f32),
            pltpu.VMEM((NX * ROWS, WIDTH), f32),
            pltpu.VMEM((DRAFTS, 128), jnp.int32),
            pltpu.VMEM((NX, ROWS, 128), jnp.int32),
            pltpu.VMEM((8, 128), f32),
            pltpu.VMEM((NZ - 1, 8, 128), f32),
            pltpu.VMEM((NX, 8, 128), f32),
            pltpu.VMEM((NX * NY - 1, 8, 128), f32),
            pltpu.VMEM((8, 128), f32),
            pltpu.VMEM((8, 128), f32),
            dma, dma, dma, dma, dma,
            dma((9,)), dma((9,)), dma((15,)), dma((15,)),
            dma((3, REGION)), dma((3, REGION)), dma((27,)), dma((3,)), dma((3,)),
            dma((2,)), dma((2,)), dma, dma,
            regular, regular, regular,
        ],
        compiler_params=pltpu.CompilerParams(
            collective_id=0, has_side_effects=True, vmem_limit_bytes=20 * 2**20
        ),
        name="verify",
    )(*[pltpu.with_memory_space_constraint(v, pltpu.HBM) for v in (hidden, head_weight, drafts.T)])
    log_norm, draft_logprob, expected, z_loss = pl.pallas_call(
        finish_kernel,
        out_shape=[
            jax.ShapeDtypeStruct((POSITIONS, 16), f32),
            jax.ShapeDtypeStruct((DRAFTS, 16), f32),
            jax.ShapeDtypeStruct((1, 16), f32),
            jax.ShapeDtypeStruct((1, 1), f32),
        ],
        in_specs=[vmem, vmem],
        out_specs=[vmem] * 4,
        compiler_params=pltpu.CompilerParams(vmem_limit_bytes=2**20),
        name="finish",
    )(packed, cutoffs.T)
    return log_norm.T, draft_logprob.T, expected.reshape(16), z_loss.reshape(())


def solution(mesh):
    split = Mesh(mesh.devices.reshape(NX, 2, NY, NZ), AXES)
    dp, everything = ("x", "core"), ("x", "core", "y", "z")
    return jax.shard_map(
        local,
        mesh=split,
        in_specs=(P(dp, None), P(None, everything), P(), P(dp, None)),
        out_specs=(P(dp, None), P(dp, None), P(dp), P()),
        check_vma=False,
    )
```

```python
import functools

import jax
import jax.numpy as jnp
from jax import lax
from jax.experimental import pallas as pl
from jax.experimental.pallas import tpu as pltpu
from jax.sharding import Mesh
from jax.sharding import PartitionSpec as P

DRAFTS = 4
POSITIONS = 5
AXES = ("x", "core", "y", "z")
NX, NY, NZ = 4, 8, 8
MESH = pl.DeviceIdType.MESH

SOFT_CAP = 30.0
Z_WEIGHT = 0.001

ROWS = 80
WIDTH = 512
TILE = 256
TILES = 18
REGION = 3
DIRECT = 4 * REGION
PAIR = 2
BEHIND = (0, 1, 3, 2)


def column_to_row(column, rows):
    at = lax.broadcasted_iota(jnp.int32, (rows, 128), 0)
    lane = lax.broadcasted_iota(jnp.int32, (rows, 128), 1)
    return jnp.sum(jnp.where(at == lane, column, 0.0), axis=0, keepdims=True)


def verify_kernel(
    hidden, weight, drafts, out,
    held, own_w, partner_w, acc_own, acc_partner, wanted, ids, part, both, z_in, xy_out, xy_in, result,
    load_sem, small_sem, w_sem, w_send, w_recv, color_recv, color_send, direct_recv, direct_send,
    near_recv, far_recv, plane_send, shared_recv, shared_send, red_send, red_recv, hand_send, hand_recv, fin_send, fin_recv, round_a, round_b, round_c,
):
    x, core, y, z = (lax.axis_index(a) for a in AXES)
    def ahead(n):
        return lax.rem(x + n + NX, NX)

    def at(dx=0, dy=0, dz=0):
        return (
            ahead(dx) if dx else x,
            core,
            lax.rem(y + dy + NY, NY) if dy else y,
            lax.rem(z + dz + NZ, NZ) if dz else z,
        )

    partner = (x, 1 - core, y, z)
    front, back = at(dx=1), at(dx=-1)
    colour = lax.rem(y + 2 * z, 4)
    mine = REGION * colour
    sent = []

    def remote(src, dst, send, recv, to):
        copy = pltpu.make_async_remote_copy(
            src_ref=src, dst_ref=dst, send_sem=send, recv_sem=recv, device_id=to, device_id_type=MESH
        )
        copy.start()
        return copy

    def signal(sem, peers):
        for peer in peers:
            pl.semaphore_signal(sem, inc=1, device_id=peer, device_id_type=MESH)
        return len(peers)

    neighbours = [front, back, at(dy=1), at(dy=-1), at(dz=1), at(dz=-1)]
    barrier = pltpu.get_barrier_semaphore()
    greeted = signal(barrier, neighbours + [partner])

    for t in range(TILES):
        pltpu.make_async_copy(hidden.at[:, pl.ds(t * TILE, TILE)], held.at[t, 0], load_sem).start()
    load_ids = pltpu.make_async_copy(drafts, wanted, small_sem)
    load_ids.start()
    load_w = pltpu.make_async_copy(weight, own_w, w_sem)
    load_w.start()
    pltpu.make_async_copy(held.at[:, 0], held.at[:, 0], load_sem).wait()
    pl.semaphore_wait(barrier, greeted)

    color_in = {}
    for i, (to, place, t) in enumerate(
        [(front, 1, 0), (back, 2, 2), (front, 1, 1), (back, 2, 0), (front, 1, 2), (back, 2, 1)]
    ):
        copy = remote(held.at[mine + t, 0], held.at[mine + t, place], color_send.at[i], color_recv.at[i], to)
        color_in[place, t] = copy
        sent.append(copy)

    direct_in = {}

    def direct(to, source, place, t, key=None):
        i = len(direct_in)
        copy = remote(
            held.at[DIRECT + t, source], held.at[DIRECT + t, place], direct_send.at[i], direct_recv.at[i], to
        )
        direct_in[place, t if key is None else key] = copy
        sent.append(copy)

    parity = lax.rem(z, 2)
    over_x, over_z = 2 * PAIR + parity, 2 * PAIR + 1 - parity
    direct(front, 0, 1, over_x, "x")
    direct(back, 0, 2, over_x, "x")
    low, high = range(PAIR), range(PAIR, 2 * PAIR)
    for i in range(PAIR):
        direct(front, 0, 1, low[i])
        direct(back, 0, 2, high[i])
    w_copy = remote(weight, partner_w, w_send, w_recv, partner)
    sent.append(w_copy)

    signal(round_a, neighbours)

    load_ids.wait()
    row = lax.broadcasted_iota(jnp.int32, (ROWS, 128), 0)
    lane = lax.broadcasted_iota(jnp.int32, (ROWS, 128), 1)
    chosen = wanted[...].astype(jnp.float32)
    bonus = lax.rem(lax.broadcasted_iota(jnp.int32, (ROWS, 1), 0), POSITIONS) == DRAFTS
    for place in range(NX):
        block = 2 * ahead(-BEHIND[place]) + core
        spread = jnp.zeros((ROWS, 128), jnp.float32)
        for p in range(DRAFTS):
            here = row + ROWS * block == lane * POSITIONS + p
            spread += jnp.where(here, chosen[p : p + 1], 0.0)
        found = jnp.sum(spread, axis=1, keepdims=True)
        ids[place] = jnp.broadcast_to(jnp.where(bonus, -1.0, found), (ROWS, 128)).astype(jnp.int32)

    plane_count = [0]

    def forward(place, t):
        piece = held.at[mine + t, place]
        toward = at(dz=1) if t < 2 else at(dz=-1)
        recv = far_recv if place == 3 else near_recv
        for k, to in ((0, at(dy=1)), (1, at(dy=-1)), (2, toward)):
            sent.append(remote(piece, piece, plane_send.at[plane_count[0]], recv.at[k, t], to))
            plane_count[0] += 1

    relays = {(1, 0): front, (2, 2): back, (1, 1): front}
    for place, t in [(1, 0), (2, 2), (1, 1), (2, 0), (1, 2), (2, 1)]:
        color_in[place, t].wait_recv()
        if (place, t) in relays:
            i = 6 + t
            copy = remote(
                held.at[mine + t, place], held.at[mine + t, 3], color_send.at[i], color_recv.at[i], relays[place, t]
            )
            color_in[3, t] = copy
            sent.append(copy)
        forward(place, t)

    def share(place):
        piece = held.at[DIRECT + over_x, place]
        to = at(dz=-1) if place == 2 else at(dz=1)
        sent.append(remote(piece, piece, shared_send.at[place - 1], shared_recv.at[place - 1], to))

    direct_in[1, "x"].wait_recv()
    share(1)
    direct_in[2, "x"].wait_recv()
    direct(back, 2, 3, over_x, "x")
    share(2)
    for i in range(PAIR):
        direct(front, 0, 1, high[i])
        direct(back, 0, 2, low[i])
    pl.semaphore_wait(round_a, len(neighbours))
    count_b = signal(round_b, [at(dy=2), at(dy=-2), at(dz=2), at(dz=-2)])
    for i in range(PAIR):
        direct_in[1, low[i]].wait_recv()
        direct(front, 1, 3, low[i])
        direct_in[2, high[i]].wait_recv()
        direct(back, 2, 3, high[i])
    for t in (0, 2, 1):
        color_in[3, t].wait_recv()
        forward(3, t)
    direct_in[3, "x"].wait_recv()
    share(3)
    pl.semaphore_wait(round_b, count_b)
    count_c = signal(round_c, [at(dx=1), at(dx=-1), at(dx=2)])

    load_w.wait()
    w_copy.wait_recv()
    near, far = (0, 3), (3, 1)

    def multiply(span, tiles, start=False):
        first, count = span
        rows = pl.ds(first * ROWS, count * ROWS)
        for weights, total in ((own_w, acc_own), (partner_w, acc_partner)):
            value = None if start else total[rows, :]
            for t in tiles:
                depth = pl.ds(pl.multiple_of(t * TILE, TILE), TILE)
                product = jnp.dot(
                    held[t, pl.ds(first, count)].reshape(count * ROWS, TILE),
                    weights[depth, :],
                    preferred_element_type=jnp.float32,
                )
                value = product if value is None else value + product
            total[rows, :] = value

    def arrived(t, span, sem):
        piece = held.at[t, pl.ds(*span)]
        pltpu.make_async_copy(piece, piece, sem).wait()

    vocab = y * NZ + z
    columns = lax.broadcasted_iota(jnp.int32, (ROWS, 128), 1)

    def summed(place):
        exp_sum = jnp.zeros((ROWS, 128), jnp.float32)
        pick_sum = jnp.zeros((ROWS, 128), jnp.float32)
        for total, at_core in ((acc_own, core), (acc_partner, 1 - core)):
            offset = ((2 * x + at_core) * (NY * NZ) + vocab) * WIDTH
            for j in range(WIDTH // 128):
                logits = total[pl.ds(place * ROWS, ROWS), pl.ds(j * 128, 128)]
                capped = SOFT_CAP * jnp.tanh(logits * (1.0 / SOFT_CAP))
                exp_sum += jnp.exp(capped)
                pick_sum += jnp.where(columns + (offset + j * 128) == ids[place], capped, 0.0)
        k = BEHIND[place]
        part[pl.ds(k, 1), :] = column_to_row(jnp.sum(exp_sum, axis=1, keepdims=True), ROWS)
        part[pl.ds(NX + k, 1), :] = column_to_row(jnp.sum(pick_sum, axis=1, keepdims=True), ROWS)

    def region(shift):
        return REGION * lax.rem(colour + shift, 4)

    own_tiles = [mine + t for t in range(REGION)]
    multiply(near, own_tiles, start=True)
    multiply(far, own_tiles, start=True)
    sides = ((2, 2), (0, 3), (1, 1))
    for k, shift in sides:
        tiles = [region(shift) + t for t in range(REGION)]
        for t in range(REGION):
            arrived(tiles[t], (1, 2), near_recv.at[k, t])
        multiply(near, tiles)
    for place in (1, 2):
        arrived(DIRECT + over_z, (place, 1), shared_recv.at[place - 1])
    for group, place in ((low, 2), (high, 1)):
        for t in group:
            direct_in[place, t].wait_recv()
    multiply(near, [DIRECT + t for t in range(2 * PAIR + 2)])
    tiles = [region(2) + t for t in range(REGION)]
    for t in range(REGION):
        arrived(tiles[t], (3, 1), far_recv.at[2, t])
    multiply(far, tiles)
    pl.semaphore_wait(round_c, count_c)
    for place in (0, 1, 2):
        summed(place)
    for i, t in enumerate((0, 2, 1)):
        tiles = []
        for group in (low, high) if i < PAIR else ():
            direct_in[3, group[i]].wait_recv()
            tiles.append(DIRECT + group[i])
        if i == PAIR:
            arrived(DIRECT + over_z, (3, 1), shared_recv.at[2])
            tiles += [DIRECT + 2 * PAIR, DIRECT + 2 * PAIR + 1]
        for k, shift in sides[1:]:
            tiles.append(region(shift) + t)
            arrived(tiles[-1], (3, 1), far_recv.at[k, t])
        multiply(far, tiles)
    summed(3)

    hand_over = pltpu.make_async_remote_copy(
        src_ref=part, dst_ref=both.at[1], send_sem=hand_send, recv_sem=hand_recv, device_id=partner, device_id_type=MESH
    )
    hand_back = pltpu.make_async_remote_copy(
        src_ref=result, dst_ref=out, send_sem=fin_send, recv_sem=fin_recv, device_id=partner, device_id_type=MESH
    )
    used = pl.ds(0, NX + 1)

    @pl.when(core == 0)
    def _():
        hand_over.start()

    @pl.when(core == 1)
    def _():
        both[0] = part[...]
        hand_over.wait_recv()
        for d in sorted(range(1, NZ), key=lambda d: -min(d, NZ - d)):
            remote(both, z_in.at[d - 1], red_send.at[0], red_recv.at[0], at(dz=d))
        pltpu.make_async_copy(z_in, z_in, red_recv.at[0]).wait()
        plane = both[...] + jnp.sum(z_in[...], axis=0)
        for a in range(NX):
            k = NX + (-a) % NX
            for h in range(2):
                xy_out[a, h, 0:NX] = plane[h, 0:NX]
                xy_out[a, h, NX : NX + 1] = plane[h, k : k + 1]
        pairs = [(a, b) for a in range(NX) for b in range(NY) if a or b]
        for a, b in sorted(pairs, key=lambda p: -min(p[0], NX - p[0]) - min(p[1], NY - p[1])):
            piece, into = xy_out.at[a, :, used], xy_in.at[a * NY + b - 1, :, used]
            remote(piece, into, red_send.at[1], red_recv.at[1], at(dx=a, dy=b))
        pltpu.make_async_copy(xy_in.at[:, :, used], xy_in.at[:, :, used], red_recv.at[1]).wait()
        valid = lax.broadcasted_iota(jnp.int32, (1, 128), 1) < ROWS
        kept, squares = [], jnp.zeros((1, 128), jnp.float32)
        for h in range(2):
            from_x = []
            for a in range(NX):
                first = max(a * NY - 1, 0)
                count = NY if a else NY - 1
                value = jnp.sum(xy_in[pl.ds(first, count), h, 0 : NX + 1], axis=0)
                from_x.append(value + xy_out[0, h, 0 : NX + 1] if a == 0 else value)
            for slot in range(NX):
                value = functools.reduce(
                    jnp.add, [from_x[a][(slot - a) % NX : (slot - a) % NX + 1] for a in range(NX)]
                )
                log = jnp.log(jnp.where(valid, value, 1.0))
                squares += log * log
                if slot == 0:
                    kept.append((log, functools.reduce(jnp.add, [v[NX : NX + 1] for v in from_x])))
        for into, (log, picked) in ((result, kept[1]), (out, kept[0])):
            into[pl.ds(0, 1), :] = log
            into[pl.ds(1, 1), :] = picked
            into[pl.ds(2, 1), :] = squares
            into[pl.ds(3, 5), :] = jnp.zeros((5, 128), jnp.float32)
            if into is result:
                hand_back.start()
        pltpu.make_async_copy(z_in, z_in, red_send.at[0]).wait()
        pltpu.make_async_copy(xy_in.at[:, :, used], xy_in.at[:, :, used], red_send.at[1]).wait()
        hand_back.wait_send()

    for copy in sent:
        copy.wait_send()

    @pl.when(core == 0)
    def _():
        hand_over.wait_send()
        hand_back.wait_recv()


def finish_kernel(packed, cutoffs, log_norm, draft_logprob, expected, z_loss):
    seqs = 16
    at = lax.broadcasted_iota(jnp.int32, (seqs, 128), 0)
    lane = lax.broadcasted_iota(jnp.int32, (seqs, 128), 1)
    logs, picked, squares = packed[0:1], packed[1:2], packed[2:3]
    product = jnp.ones((1, seqs), jnp.float32)
    total = jnp.zeros((1, seqs), jnp.float32)
    for p in range(POSITIONS):
        here = lane == at * POSITIONS + p

        def of(values):
            return column_to_row(jnp.sum(jnp.where(here, values, 0.0), axis=1, keepdims=True), seqs)[:, 0:seqs]

        log_p = of(logs)
        log_norm[p : p + 1, :] = log_p
        if p < DRAFTS:
            draft = of(picked) - log_p
            draft_logprob[p : p + 1, :] = draft
            limit = cutoffs[p : p + 1, :].astype(jnp.float32) * (1.0 / 1024.0)
            product = product * (1.0 / (1.0 + jnp.exp(limit - draft)))
            total = total + product
    expected[...] = total
    z_loss[...] = jnp.sum(squares, axis=1, keepdims=True) * (Z_WEIGHT / (128 * POSITIONS))


def local(hidden, head_weight, drafts, cutoffs):
    f32, bf16 = jnp.float32, jnp.bfloat16
    dma, regular = pltpu.SemaphoreType.DMA, pltpu.SemaphoreType.REGULAR
    vmem = pl.BlockSpec(memory_space=pltpu.VMEM)
    hbm = pl.BlockSpec(memory_space=pltpu.HBM)
    packed = pl.pallas_call(
        verify_kernel,
        out_shape=jax.ShapeDtypeStruct((8, 128), f32),
        in_specs=[hbm, hbm, hbm],
        out_specs=vmem,
        scratch_shapes=[
            pltpu.VMEM((TILES, NX, ROWS, TILE), bf16),
            pltpu.VMEM((TILES * TILE, WIDTH), bf16),
            pltpu.VMEM((TILES * TILE, WIDTH), bf16),
            pltpu.VMEM((NX * ROWS, WIDTH), f32),
            pltpu.VMEM((NX * ROWS, WIDTH), f32),
            pltpu.VMEM((DRAFTS, 128), jnp.int32),
            pltpu.VMEM((NX, ROWS, 128), jnp.int32),
            pltpu.VMEM((8, 128), f32),
            pltpu.VMEM((2, 8, 128), f32),
            pltpu.VMEM((NZ - 1, 2, 8, 128), f32),
            pltpu.VMEM((NX, 2, 8, 128), f32),
            pltpu.VMEM((NX * NY - 1, 2, 8, 128), f32),
            pltpu.VMEM((8, 128), f32),
            dma, dma, dma, dma, dma,
            dma((9,)), dma((9,)), dma((15,)), dma((15,)),
            dma((3, REGION)), dma((3, REGION)), dma((27,)), dma((3,)), dma((3,)),
            dma((2,)), dma((2,)), dma, dma, dma, dma,
            regular, regular, regular,
        ],
        compiler_params=pltpu.CompilerParams(
            collective_id=0, has_side_effects=True, vmem_limit_bytes=20 * 2**20
        ),
        name="verify",
    )(*[pltpu.with_memory_space_constraint(v, pltpu.HBM) for v in (hidden, head_weight, drafts.T)])
    log_norm, draft_logprob, expected, z_loss = pl.pallas_call(
        finish_kernel,
        out_shape=[
            jax.ShapeDtypeStruct((POSITIONS, 16), f32),
            jax.ShapeDtypeStruct((DRAFTS, 16), f32),
            jax.ShapeDtypeStruct((1, 16), f32),
            jax.ShapeDtypeStruct((1, 1), f32),
        ],
        in_specs=[vmem, vmem],
        out_specs=[vmem] * 4,
        compiler_params=pltpu.CompilerParams(vmem_limit_bytes=2**20),
        name="finish",
    )(packed, cutoffs.T)
    return log_norm.T, draft_logprob.T, expected.reshape(16), z_loss.reshape(())


def solution(mesh):
    split = Mesh(mesh.devices.reshape(NX, 2, NY, NZ), AXES)
    dp, everything = ("x", "core"), ("x", "core", "y", "z")
    return jax.shard_map(
        local,
        mesh=split,
        in_specs=(P(dp, None), P(None, everything), P(), P(dp, None)),
        out_specs=(P(dp, None), P(dp, None), P(dp), P()),
        check_vma=False,
    )
```
